32 devices in a mesh: grp: 2 (over x), freq: 16 (over z, y, core).
Axes of the slice: x: 2, y: 2, z: 4, core: 2. Of those that a mesh axis runs over, the one named last changes fastest.
Arguments:
- start_field: bfloat16 [512, 384, 512], P(('grp', 'freq')), parts along dimension 0, may hold values from -2.390625 to 2.390625
- recorded: bfloat16 [32, 384, 4, 128], P(('grp', 'freq')), parts along dimension 0, may hold values from -6 to 6
- multiples: bfloat16 [32, 4, 3, 64, 128], P(('grp', 'freq')), parts along dimension 0, may hold values from -0.3125 to 0.3125
- block_index: int32 [4, 3], replicated, may hold values from 0 to 3, all different within a row
- radius: int32 [512, 384], P(('grp', 'freq')), parts along dimension 0, may hold values from 0 to 4
Outputs:
- field: float32 [512, 384, 512], P(('grp', 'freq')), parts along dimension 0
- residual: float32 [32, 384, 4, 128], P(('grp', 'freq')), parts along dimension 0
The draws below stay inside these ranges and needn't reach their ends.
There are 2 independent parts, one for each index of `grp`. The reference program is written for one: setup_inputs(seed, part) draws one part's arguments, and reference() takes and returns one part's arrays. A program takes and returns all parts, laid end to end along the dimension named above; an argument that names none is the same for every part. Nothing has to cross between parts.
Inputs may be any that keep to these rules, and one draw needn't show every extreme that they name: `block_index`: each row names 3 different source blocks, and every block is named by some row.
All inputs are finite; a program needn't handle non-finite values.
Results may differ from the reference program's by a relative error of at most 0.004.
Values may be sent and summed in bfloat16 or wider, within the bound.
A program may use at most 64 MiB of HBM per device.

```python
import math
import jax
import jax.numpy as jnp
from jax import lax

NB = 4
BS = 64
BANDS = 3
NT = 512
RADIUS = 4
ITERS = 2
RECV = 384
S = 256
FREQ = 16


def draw_radius(key, part):
    uniform_pick = jax.random.randint(key, (S, RECV), 0, RADIUS + 1)
    source_ids = jnp.arange(S, dtype=jnp.int32)[:, None]
    receiver_ids = jnp.arange(RECV, dtype=jnp.int32)[None, :]
    return jnp.where((source_ids * 7 + receiver_ids) % 11 == 0, RADIUS, uniform_pick).astype(jnp.int32)


def shard_levels(key, shape, shards, least, top_value):
    factor_of, own = 1.0, jax.random.fold_in(key, 6)
    for dim, blocks in shards:
        steps = jnp.exp(jax.random.uniform(jax.random.fold_in(own, dim), (blocks,), jnp.float32, least / len(shards), top_value / len(shards)))
        factor_of = factor_of * jnp.repeat(steps, shape[dim] // blocks).reshape([-1 if axis == dim else 1 for axis in range(len(shape))])
    return factor_of


def picks_of(own_key, rows, amount, top, lift):
    order = jax.random.permutation(jax.random.fold_in(own_key, 1), amount)
    boost = order
    for power in range(3):
        boost = boost * boost // amount
    boost = boost * lift // amount
    tickets = jax.random.randint(jax.random.fold_in(own_key, 2), (rows, amount), 0, 4096) + boost
    fixed_rows = jax.random.permutation(jax.random.fold_in(own_key, 3), rows)[jnp.arange(amount) % rows]
    tickets = jnp.where(jnp.arange(rows)[:, None] == fixed_rows[None, :], 1 << 14, tickets)
    merit = tickets * amount + jnp.arange(amount)
    return lax.top_k(merit.astype(jnp.int32), top)[1].astype(jnp.int32)


def bell_draw(key, extent, spread, most, cuts=(), kind=jnp.bfloat16):
    array = jax.random.normal(key, extent, jnp.float32) * spread
    if len(cuts) > 0:
        array = shard_levels(key, extent, cuts, -0.22, 0.18) * array
    return jnp.clip(array, min=-most, max=most).astype(kind)


def setup_inputs(seed: int = 0, part: int = 0) -> dict:
    arg_keys = jax.random.split(jax.random.key(seed), 6)
    own_keys = jax.random.split(jax.random.fold_in(arg_keys[5], part), 6)
    start_field = bell_draw(own_keys[0], (S, RECV, NT), 0.3, 2.390625, ((0, 16),))
    recorded = bell_draw(own_keys[1], (FREQ, RECV, NB, 2 * BS), 1.0, 6.0, ((0, 16),))
    multiples = bell_draw(own_keys[2], (FREQ, NB, BANDS, BS, 2 * BS), (2 * BANDS * BS) ** -0.5, 0.3125, ((0, 16),))
    block_index = picks_of(arg_keys[3], NB, NB, BANDS, 0)
    radius = draw_radius(jax.random.fold_in(jax.random.fold_in(arg_keys[5], part), 71), part)
    return dict(start_field=start_field, recorded=recorded, multiples=multiples, block_index=block_index, radius=radius)


step_size = 0.5
shrinkage = 0.05

def dft_table(freq_count):
    sample_ids = jnp.arange(NT, dtype=jnp.int32)
    bin_ids = jnp.arange(freq_count, dtype=jnp.int32) + 1
    phases = sample_ids[:, None] * bin_ids[None, :] % NT
    angles = phases.astype(jnp.float32) * (2.0 * math.pi / NT)
    stacked = jnp.stack([jnp.cos(angles), -jnp.sin(angles)], axis=-1)
    return stacked.reshape(NT, 2 * freq_count) / math.sqrt(NT)

def embed_complex(multiples):
    real_part = multiples[..., :BS]
    imag_part = multiples[..., BS:]
    upper_rows = jnp.concatenate([real_part, imag_part], axis=-1)
    lower_rows = jnp.concatenate([-imag_part, real_part], axis=-1)
    return jnp.concatenate([upper_rows, lower_rows], axis=-2)

def owner_layout(arrived, freq_count):
    shaped = arrived.reshape(freq_count, 2, NB, BS, arrived.shape[2])
    return shaped.transpose(0, 4, 2, 1, 3).reshape(freq_count, arrived.shape[2], NB, 2 * BS)

def trace_layout(backward, freq_count):
    shaped = backward.reshape(freq_count, backward.shape[1], NB, 2, BS)
    return shaped.transpose(0, 3, 2, 4, 1).reshape(2 * freq_count, NB * BS, backward.shape[1])

def smooth_along(extended, radius, rows_out, along):
    shares = 1.0 / (2.0 * radius.astype(jnp.float32) + 1.0)
    summed = None
    for offset in range(-RADIUS, RADIUS + 1):
        weight = jnp.where(abs(offset) <= radius, shares, 0.0)
        if along == 0:
            weight = weight[:, :, None]
        else:
            weight = weight[None, :, :]
        piece = lax.slice_in_dim(extended, RADIUS + offset, RADIUS + offset + rows_out, axis=along)
        term = weight * piece.astype(jnp.float32)
        summed = term if summed is None else summed + term
    return summed

def reference(start_field, recorded, multiples, block_index, radius):
    basis = dft_table(FREQ)
    operator = embed_complex(multiples).astype(jnp.float32)
    field = start_field.astype(jnp.float32)
    residual = None
    for sweep in range(ITERS):
        spectra = jnp.einsum('srt,tc->csr', field, basis, precision=lax.Precision.HIGHEST).astype(jnp.bfloat16)
        spectra = lax.optimization_barrier(spectra)
        owned = owner_layout(spectra, FREQ).astype(jnp.float32)
        predicted = []
        for out_block in range(NB):
            summed = jnp.zeros((FREQ, RECV, 2 * BS), jnp.float32)
            for band_id in range(BANDS):
                source = owned[:, :, block_index[out_block, band_id]]
                summed = summed + jnp.einsum('frc,fcd->frd', source, operator[:, out_block, band_id])
            predicted.append(summed)
        residual = recorded.astype(jnp.float32) - jnp.stack(predicted, axis=2)
        narrow = lax.optimization_barrier(residual.astype(jnp.bfloat16)).astype(jnp.float32)
        backward = jnp.zeros((FREQ, RECV, NB, 2 * BS), jnp.float32)
        for out_block in range(NB):
            for band_id in range(BANDS):
                contrib = jnp.einsum('frd,fcd->frc', narrow[:, :, out_block], operator[:, out_block, band_id])
                backward = backward.at[:, :, block_index[out_block, band_id]].add(contrib)
        returned = lax.optimization_barrier(trace_layout(backward.astype(jnp.bfloat16), FREQ)).astype(jnp.float32)
        gradient = jnp.einsum('csr,tc->srt', returned, basis, precision=lax.Precision.HIGHEST)
        extended = jnp.pad(gradient, ((RADIUS, RADIUS), (0, 0), (0, 0)))
        smoothed = smooth_along(extended, radius, S, 0)
        update = field + step_size * smoothed
        field = jnp.sign(update) * jnp.maximum(jnp.abs(update) - shrinkage, 0.0)
    return (field, residual)
```

```python
import functools
import math

import jax
import jax.numpy as jnp
import numpy as np
from jax import lax
from jax.experimental import pallas as pl
from jax.experimental.pallas import tpu as pltpu
from jax.sharding import PartitionSpec as P

NB = 4
BS = 64
BANDS = 3
RADIUS = 4
PAD = 8

step_size = 0.5
shrinkage = 0.05

BF16 = jnp.bfloat16
F32 = jnp.float32


def dft_table(freq_count, samples):
    phases = (np.arange(samples)[:, None] * (np.arange(freq_count) + 1)[None, :]) % samples
    angles = phases.astype(np.float64) * (2.0 * math.pi / samples)
    stacked = np.stack([np.cos(angles), -np.sin(angles)], axis=-1)
    return (stacked.reshape(samples, 2 * freq_count) / math.sqrt(samples)).astype(np.float32)


def halves(table):
    high = jnp.asarray(table).astype(BF16)
    low = (jnp.asarray(table) - high.astype(F32)).astype(BF16)
    return high, low


def soft(update):
    return update - jnp.clip(update, -shrinkage, shrinkage)


def nt_dot(a, b):
    return lax.dot_general(a, b, (((1,), (1,)), ((), ())), preferred_element_type=F32)


def tn_dot(a, b):
    return lax.dot_general(a, b, (((0,), (0,)), ((), ())), preferred_element_type=F32)


def build_operator(block_ref, multiples_ref, inner, local_src):
    parts = BS // local_src
    for f in range(multiples_ref.shape[0]):
        for j in range(NB):
            terms = [multiples_ref[f, j, b].astype(F32) for b in range(BANDS)]
            for m in range(NB):
                block = None
                for b in range(BANDS):
                    term = terms[b] * jnp.where(block_ref[j, b] == m, 1.0, 0.0)
                    block = term if block is None else block + term
                turned = jnp.concatenate([-block[:, BS:], block[:, :BS]], axis=1)
                for q in range(parts):
                    for c, half in enumerate((block, turned)):
                        row = ((m * parts + q) * 2 + c) * local_src
                        piece = half[q * local_src : (q + 1) * local_src]
                        inner[f, row : row + local_src, j * 2 * BS : (j + 1) * 2 * BS] = piece.astype(BF16)


def sweeps_kernel(
    devices, chunks, width,
    block_hbm, start_hbm, recorded_hbm, multiples_hbm, radius_hbm, analysis_hbm, synthesis_hbm,
    field_ref, last_ref, residual_ref,
    field, wide, flat, near, radii, spans, shares, given, inner, out_slabs, in_slabs, back_slabs, edge_slabs,
    block_ref, recorded_ref, multiples_ref, radius_ref, analysis_ref, synthesis_ref,
    load_sem, send_sem, recv_sem, table_sem, radii_send, radii_recv,
):
    me = lax.axis_index("freq")
    local_src = start_hbm.shape[0]
    local_freq = multiples_hbm.shape[0]
    rows = analysis_ref.shape[0] // 2
    per = max(1, 8 // local_src)
    block = per * local_src
    block_cols = 2 * BS

    def load(c):
        return pltpu.make_async_copy(start_hbm.at[:, pl.ds(c * width, width), :], field.at[c], load_sem.at[c])

    load(0).start()
    tables = [
        pltpu.make_async_copy(source, target, table_sem.at[n])
        for n, (source, target) in enumerate(
            (
                (analysis_hbm, analysis_ref),
                (block_hbm, block_ref),
                (multiples_hbm, multiples_ref),
                (radius_hbm, radius_ref),
                (recorded_hbm, recorded_ref),
                (synthesis_hbm, synthesis_ref),
            )
        )
    ]
    tables[0].start()
    for c in range(1, chunks):
        load(c).start()
    for table in tables[1:]:
        table.start()
    barrier = pltpu.get_barrier_semaphore()
    for shift in range(1, devices):
        pl.semaphore_signal(
            barrier, inc=1, device_id={"freq": lax.rem(me + shift, devices)}, device_id_type=pl.DeviceIdType.MESH
        )

    def exchange(phase, c, sources, targets):
        slot = phase * chunks + c
        place = (phase // 2) * chunks + c

        def send(step, carry):
            peer = lax.rem(me + step, devices)
            pltpu.make_async_remote_copy(
                src_ref=sources.at[place, peer],
                dst_ref=targets.at[place, me],
                send_sem=send_sem.at[slot],
                recv_sem=recv_sem.at[slot],
                device_id={"freq": peer},
                device_id_type=pl.DeviceIdType.MESH,
            ).start()
            return carry

        lax.fori_loop(1, devices, send, 0)
        targets[place, me] = sources[place, me]

    def await_all(phase, c, refs, sems):
        whole = refs.at[(phase // 2) * chunks + c, pl.ds(0, devices - 1)]
        pltpu.make_async_copy(whole, whole, sems.at[phase * chunks + c]).wait()

    side = radii.shape[0]
    planes = devices // side
    plane, spot = me // side, lax.rem(me, side)

    def radii_across(step):
        return pltpu.make_async_remote_copy(
            src_ref=radii.at[spot, plane],
            dst_ref=radii.at[spot, plane],
            send_sem=radii_send.at[0],
            recv_sem=radii_recv.at[0],
            device_id={"freq": lax.rem(plane + step, planes) * side + spot},
            device_id_type=pl.DeviceIdType.MESH,
        )

    def radii_around(step):
        return pltpu.make_async_remote_copy(
            src_ref=radii.at[spot],
            dst_ref=radii.at[spot],
            send_sem=radii_send.at[1],
            recv_sem=radii_recv.at[1],
            device_id={"freq": plane * side + lax.rem(spot + step, side)},
            device_id_type=pl.DeviceIdType.MESH,
        )

    def await_radii(stage, sems):
        several = radii.at[0, pl.ds(0, planes - 1)] if stage == 0 else radii.at[pl.ds(0, side - 1)]
        pltpu.make_async_copy(several, several, sems.at[stage]).wait()

    def analyse(s, samples):
        both = nt_dot(analysis_ref[...], samples)
        wide[pl.ds(s, rows, stride=local_src), :] = both[:rows] + both[rows:]

    def ship(sweep, c):
        slabs = wide[...].reshape(devices, local_freq * 2 * local_src, width)
        out_slabs[sweep * chunks + c] = slabs.astype(BF16)
        if sweep == 0 and c == 0:
            tables[3].wait()
            radii[spot, plane] = radius_ref[...].astype(F32).astype(BF16)
            pl.semaphore_wait(barrier, devices - 1)
            for step in range(1, planes):
                radii_across(step).start()
        exchange(2 * sweep, c, out_slabs, in_slabs)

    def own(sweep, c):
        await_all(2 * sweep, c, in_slabs, recv_sem)
        arrived = in_slabs[sweep * chunks + c].astype(F32)
        span_lanes = pl.ds(c * width, width)
        for f in range(local_freq):
            part = arrived[:, f * 2 * local_src : (f + 1) * 2 * local_src]
            owned = part.reshape(devices * 2 * local_src, width).T.astype(BF16)
            predicted = jnp.dot(owned, inner[f], preferred_element_type=F32)
            given[...] = recorded_ref[f, pl.ds(c * width * NB, width * NB), :].astype(F32)
            narrow = []
            for j in range(NB):
                left = given[pl.ds(j, width, stride=NB), :] - predicted[:, j * block_cols : (j + 1) * block_cols]
                if sweep == 1:
                    residual_ref[f, pl.ds(c * width * NB + j, width, stride=NB), :] = left
                narrow.append(left.astype(BF16))
            back = nt_dot(inner[f], jnp.concatenate(narrow, axis=1))
            for p in range(devices):
                for h in range(2):
                    at = (2 * p + h) * local_src
                    near[h, PAD + p * local_src : PAD + (p + 1) * local_src, :] = back[at : at + local_src]
            if sweep == 0 and c == 0 and f == 0:
                gather_spans()

            def smooth(g, carry):
                start = pl.multiple_of(g * block, 8)
                rows_of = pl.ds(start, block)
                span, share = spans[rows_of, span_lanes], shares[rows_of, span_lanes]
                pair = []
                for h in range(2):
                    box = near[h, pl.ds(start + PAD, block), :]
                    smoothed = box
                    for offset in range(1, RADIUS + 1):
                        box = box + (
                            near[h, pl.ds(start + PAD + offset, block), :]
                            + near[h, pl.ds(start + PAD - offset, block), :]
                        )
                        smoothed = jnp.where(span >= offset, box, smoothed)
                    pair.append(smoothed * share)
                for n in range(per):
                    slab = jnp.concatenate([half[n * local_src : (n + 1) * local_src] for half in pair], axis=0)
                    part = slice(f * 2 * local_src, (f + 1) * 2 * local_src)
                    back_slabs[sweep * chunks + c, g * per + n, part, :] = slab.astype(BF16)
                return carry

            lax.fori_loop(0, devices // per, smooth, 0, unroll=4)
        exchange(2 * sweep + 1, c, back_slabs, edge_slabs)

    def gather_spans():
        if side > 1:
            await_radii(1, radii_recv)
        for p in range(devices):
            at = p * local_src
            span = radii[p % side, p // side].astype(F32)
            spans[at : at + local_src, :] = span
            shares[at : at + local_src, :] = 1.0 / (2.0 * span + 1.0)

    def trace_side(sweep, c):
        place = sweep * chunks + c
        await_all(2 * sweep + 1, c, edge_slabs, recv_sem)
        if sweep == 1 and c == chunks - 1:
            last_ref[...] = edge_slabs[place]
            return
        flat[...] = edge_slabs[place].astype(F32).reshape(rows * local_src, width)
        lanes = pl.ds(c * width, width)

        def source(s, carry):
            spectrum = flat[pl.ds(s, rows, stride=local_src), :].astype(BF16)
            step = tn_dot(jnp.concatenate([spectrum, spectrum], axis=0), synthesis_ref[...])
            if sweep == 0:
                update = soft(field[c, s].astype(F32) + step)
                field_ref[s, lanes, :] = update
                analyse(s, update.astype(BF16))
            else:
                field_ref[s, lanes, :] = soft(field_ref[s, lanes, :] + step)
            return carry

        lax.fori_loop(0, local_src, source, 0, unroll=4)
        if sweep == 0:
            ship(1, c)

    tables[0].wait()
    for c in range(chunks):
        load(c).wait()

        def source(s, carry):
            analyse(s, field[c, s])
            return carry

        lax.fori_loop(0, local_src, source, 0, unroll=4)
        ship(0, c)
    if planes > 1:
        await_radii(0, radii_recv)
    for step in range(1, side):
        radii_around(step).start()
    for n, table in enumerate(tables):
        if n not in (0, 3):
            table.wait()
    build_operator(block_ref, multiples_ref, inner, local_src)
    for h in range(2):
        near[h, 0:PAD, :] = jnp.zeros((PAD, width), F32)
        near[h, PAD + devices * local_src :, :] = jnp.zeros((PAD, width), F32)
    for sweep in range(2):
        for c in range(chunks):
            own(sweep, c)
        for c in range(chunks):
            trace_side(sweep, c)
    for phase in range(4):
        for c in range(chunks):
            await_all(phase, c, back_slabs if phase % 2 else out_slabs, send_sem)
    if planes > 1:
        await_radii(0, radii_send)
    if side > 1:
        await_radii(1, radii_send)


def finish_kernel(
    once_ref, last_ref, residual_ref, synthesis_hbm, field_hbm, residual_hbm,
    done, flat, synthesis_ref, ready_sem, done_sem, residual_sem, table_sem,
):
    local_src, receivers, _ = once_ref.shape
    width = last_ref.shape[2]
    rows = flat.shape[0] // local_src
    start = receivers - width
    ready = pltpu.make_async_copy(once_ref.at[:, pl.ds(0, start), :], field_hbm.at[:, pl.ds(0, start), :], ready_sem)
    residual = pltpu.make_async_copy(residual_ref, residual_hbm, residual_sem)
    table = pltpu.make_async_copy(synthesis_hbm, synthesis_ref, table_sem)
    table.start()
    if start:
        ready.start()
    residual.start()
    flat[...] = last_ref[...].astype(F32).reshape(flat.shape)
    table.wait()

    def source(s, carry):
        spectrum = flat[pl.ds(s, rows, stride=local_src), :].astype(BF16)
        step = tn_dot(jnp.concatenate([spectrum, spectrum], axis=0), synthesis_ref[...])
        done[s] = soft(once_ref[s, pl.ds(start, width), :] + step)
        pltpu.make_async_copy(done.at[s], field_hbm.at[s, pl.ds(start, width), :], done_sem).start()
        return carry

    lax.fori_loop(0, local_src, source, 0, unroll=4)
    pltpu.make_async_copy(done, field_hbm.at[:, pl.ds(start, width), :], done_sem).wait()
    residual.wait()
    if start:
        ready.wait()


def on_device(devices, start_field, recorded, multiples, block_index, radius):
    local_src, receivers, samples = start_field.shape
    local_freq = recorded.shape[0]
    rows = 2 * local_freq * devices
    width = 128
    chunks = receivers // width
    table = dft_table(local_freq * devices, samples)
    analysis = jnp.concatenate(halves(table.T), axis=0)
    high, low = halves(step_size * table.T)
    synthesis = jnp.concatenate([high, low], axis=0)
    side = math.gcd(devices, 4)
    sources = devices * local_src
    vmem = pl.BlockSpec(memory_space=pltpu.VMEM)
    hbm = pl.BlockSpec(memory_space=pltpu.HBM)
    slab = pltpu.VMEM((2 * chunks, devices, local_freq * 2 * local_src, width), BF16)
    flat = pltpu.VMEM((rows * local_src, width), F32)
    field_shape = jax.ShapeDtypeStruct(start_field.shape, F32)
    residual_shape = jax.ShapeDtypeStruct((local_freq, receivers * NB, 2 * BS), F32)
    once, last, residual = pl.pallas_call(
        functools.partial(sweeps_kernel, devices, chunks, width),
        out_shape=(field_shape, jax.ShapeDtypeStruct((devices, local_freq * 2 * local_src, width), BF16), residual_shape),
        in_specs=[hbm] * 7,
        out_specs=(vmem, vmem, vmem),
        scratch_shapes=[
            pltpu.VMEM((chunks, local_src, width, samples), BF16),
            flat,
            flat,
            pltpu.VMEM((2, sources + 2 * PAD, width), F32),
            pltpu.VMEM((side, devices // side, local_src, receivers), BF16),
            pltpu.VMEM((sources, receivers), F32),
            pltpu.VMEM((sources, receivers), F32),
            pltpu.VMEM((width * NB, 2 * BS), F32),
            pltpu.VMEM((local_freq, devices * 2 * local_src, NB * 2 * BS), BF16),
            slab,
            slab,
            slab,
            slab,
            pltpu.SMEM(block_index.shape, block_index.dtype),
            pltpu.VMEM((local_freq, receivers * NB, 2 * BS), BF16),
            pltpu.VMEM(multiples.shape, BF16),
            pltpu.VMEM(radius.shape, radius.dtype),
            pltpu.VMEM(analysis.shape, BF16),
            pltpu.VMEM(synthesis.shape, BF16),
            pltpu.SemaphoreType.DMA((chunks,)),
            pltpu.SemaphoreType.DMA((4 * chunks,)),
            pltpu.SemaphoreType.DMA((4 * chunks,)),
            pltpu.SemaphoreType.DMA((6,)),
            pltpu.SemaphoreType.DMA((2,)),
            pltpu.SemaphoreType.DMA((2,)),
        ],
        compiler_params=pltpu.CompilerParams(
            collective_id=0, has_side_effects=True, vmem_limit_bytes=28 << 20
        ),
    )(
        *(
            pltpu.with_memory_space_constraint(value, pltpu.HBM)
            for value in (
                block_index, start_field, recorded.reshape(local_freq, receivers * NB, 2 * BS), multiples, radius,
                analysis, synthesis,
            )
        )
    )
    field, residual = pl.pallas_call(
        finish_kernel,
        out_shape=(field_shape, residual_shape),
        in_specs=[vmem] * 3 + [hbm],
        out_specs=(hbm, hbm),
        scratch_shapes=[
            pltpu.VMEM((local_src, width, samples), F32),
            flat,
            pltpu.VMEM(synthesis.shape, BF16),
            pltpu.SemaphoreType.DMA,
            pltpu.SemaphoreType.DMA,
            pltpu.SemaphoreType.DMA,
            pltpu.SemaphoreType.DMA,
        ],
        compiler_params=pltpu.CompilerParams(vmem_limit_bytes=12 << 20),
    )(once, last, residual, pltpu.with_memory_space_constraint(synthesis, pltpu.HBM))
    return field, residual.reshape(recorded.shape)


def solution(mesh):
    placed = (
        P(("grp", "freq"), None, None),
        P(("grp", "freq"), None, None, None),
        P(("grp", "freq"), None, None, None, None),
        P(),
        P(("grp", "freq"), None),
    )
    return jax.shard_map(
        functools.partial(on_device, mesh.shape["freq"]),
        mesh=mesh,
        in_specs=placed,
        out_specs=(P(("grp", "freq"), None, None), P(("grp", "freq"), None, None, None)),
        check_vma=False,
    )
```

```python
import functools
import math

import jax
import jax.numpy as jnp
import numpy as np
from jax import lax
from jax.experimental import pallas as pl
from jax.experimental.pallas import tpu as pltpu
from jax.sharding import PartitionSpec as P

NB = 4
BS = 64
BANDS = 3
RADIUS = 4
PAD = 8

step_size = 0.5
shrinkage = 0.05

BF16 = jnp.bfloat16
F32 = jnp.float32


def dft_table(freq_count, samples):
    phases = (np.arange(samples)[:, None] * (np.arange(freq_count) + 1)[None, :]) % samples
    angles = phases.astype(np.float64) * (2.0 * math.pi / samples)
    stacked = np.stack([np.cos(angles), -np.sin(angles)], axis=-1)
    return (stacked.reshape(samples, 2 * freq_count) / math.sqrt(samples)).astype(np.float32)


def halves(table):
    high = jnp.asarray(table).astype(BF16)
    low = (jnp.asarray(table) - high.astype(F32)).astype(BF16)
    return high, low


def soft(update):
    return update - jnp.clip(update, -shrinkage, shrinkage)


def nt_dot(a, b):
    return lax.dot_general(a, b, (((1,), (1,)), ((), ())), preferred_element_type=F32)


def tn_dot(a, b):
    return lax.dot_general(a, b, (((0,), (0,)), ((), ())), preferred_element_type=F32)


def build_operator(block_ref, multiples_ref, inner, local_src):
    parts = BS // local_src
    for f in range(multiples_ref.shape[0]):
        for j in range(NB):
            terms = [multiples_ref[f, j, b].astype(F32) for b in range(BANDS)]
            for m in range(NB):
                block = None
                for b in range(BANDS):
                    term = terms[b] * jnp.where(block_ref[j, b] == m, 1.0, 0.0)
                    block = term if block is None else block + term
                turned = jnp.concatenate([-block[:, BS:], block[:, :BS]], axis=1)
                for q in range(parts):
                    for c, half in enumerate((block, turned)):
                        row = ((m * parts + q) * 2 + c) * local_src
                        piece = half[q * local_src : (q + 1) * local_src]
                        inner[f, row : row + local_src, j * 2 * BS : (j + 1) * 2 * BS] = piece.astype(BF16)


def sweeps_kernel(
    devices, chunks, width,
    block_hbm, start_hbm, recorded_hbm, multiples_hbm, radius_hbm, analysis_hbm, synthesis_hbm,
    field_ref, last_ref, residual_ref,
    field, wide, flat, near, radii, spans, shares, given, inner, out_slabs, in_slabs, back_slabs, edge_slabs,
    block_ref, recorded_ref, multiples_ref, radius_ref, analysis_ref, synthesis_ref,
    load_sem, send_sem, recv_sem, table_sem, radii_send, radii_recv,
):
    me = lax.axis_index("freq")
    local_src, _, samples = start_hbm.shape
    local_freq = multiples_hbm.shape[0]
    rows = analysis_ref.shape[0] // 2
    per = max(1, 8 // local_src)
    block = per * local_src
    block_cols = 2 * BS

    def load(c):
        return pltpu.make_async_copy(start_hbm.at[:, pl.ds(c * width, width), :], field.at[c], load_sem.at[c])

    load(0).start()
    tables = [
        pltpu.make_async_copy(source, target, table_sem.at[n])
        for n, (source, target) in enumerate(
            (
                (analysis_hbm, analysis_ref),
                (block_hbm, block_ref),
                (multiples_hbm, multiples_ref),
                (radius_hbm, radius_ref),
                (recorded_hbm, recorded_ref),
                (synthesis_hbm, synthesis_ref),
            )
        )
    ]
    tables[0].start()
    for c in range(1, chunks):
        load(c).start()
    for table in tables[1:]:
        table.start()
    barrier = pltpu.get_barrier_semaphore()
    for shift in range(1, devices):
        pl.semaphore_signal(
            barrier, inc=1, device_id={"freq": lax.rem(me + shift, devices)}, device_id_type=pl.DeviceIdType.MESH
        )

    def exchange(phase, c, sources, targets):
        slot = phase * chunks + c
        place = (phase // 2) * chunks + c

        def send(step, carry):
            peer = lax.rem(me + step, devices)
            pltpu.make_async_remote_copy(
                src_ref=sources.at[place, peer],
                dst_ref=targets.at[place, me],
                send_sem=send_sem.at[slot],
                recv_sem=recv_sem.at[slot],
                device_id={"freq": peer},
                device_id_type=pl.DeviceIdType.MESH,
            ).start()
            return carry

        lax.fori_loop(1, devices, send, 0)
        targets[place, me] = sources[place, me]

    def await_all(phase, c, refs, sems):
        whole = refs.at[(phase // 2) * chunks + c, pl.ds(0, devices - 1)]
        pltpu.make_async_copy(whole, whole, sems.at[phase * chunks + c]).wait()

    side = radii.shape[0]
    planes = devices // side
    plane, spot = me // side, lax.rem(me, side)

    def radii_across(step):
        return pltpu.make_async_remote_copy(
            src_ref=radii.at[spot, plane],
            dst_ref=radii.at[spot, plane],
            send_sem=radii_send.at[0],
            recv_sem=radii_recv.at[0],
            device_id={"freq": lax.rem(plane + step, planes) * side + spot},
            device_id_type=pl.DeviceIdType.MESH,
        )

    def radii_around(step):
        return pltpu.make_async_remote_copy(
            src_ref=radii.at[spot],
            dst_ref=radii.at[spot],
            send_sem=radii_send.at[1],
            recv_sem=radii_recv.at[1],
            device_id={"freq": plane * side + lax.rem(spot + step, side)},
            device_id_type=pl.DeviceIdType.MESH,
        )

    def await_radii(stage, sems):
        several = radii.at[0, pl.ds(0, planes - 1)] if stage == 0 else radii.at[pl.ds(0, side - 1)]
        pltpu.make_async_copy(several, several, sems.at[stage]).wait()

    pack = math.gcd(local_src, 2)

    def analyse(s, samples):
        both = nt_dot(analysis_ref[...], samples)
        both = both[:rows] + both[rows:]
        for n in range(pack):
            wide[pl.ds(s + n, rows, stride=local_src), :] = both[:, n * width : (n + 1) * width]

    def ship(sweep, c):
        slabs = wide[...].reshape(devices, local_freq * 2 * local_src, width)
        out_slabs[sweep * chunks + c] = slabs.astype(BF16)
        if sweep == 0 and c == 0:
            tables[3].wait()
            radii[spot, plane] = radius_ref[...].astype(F32).astype(BF16)
            pl.semaphore_wait(barrier, devices - 1)
            for step in range(1, planes):
                radii_across(step).start()
        exchange(2 * sweep, c, out_slabs, in_slabs)

    def own(sweep, c):
        await_all(2 * sweep, c, in_slabs, recv_sem)
        arrived = in_slabs[sweep * chunks + c].astype(F32)
        span_lanes = pl.ds(c * width, width)
        for f in range(local_freq):
            part = arrived[:, f * 2 * local_src : (f + 1) * 2 * local_src]
            owned = part.reshape(devices * 2 * local_src, width).T.astype(BF16)
            predicted = jnp.dot(owned, inner[f], preferred_element_type=F32)
            given[...] = recorded_ref[f, pl.ds(c * width * NB, width * NB), :].astype(F32)
            narrow = []
            for j in range(NB):
                left = given[pl.ds(j, width, stride=NB), :] - predicted[:, j * block_cols : (j + 1) * block_cols]
                if sweep == 1:
                    residual_ref[f, pl.ds(c * width * NB + j, width, stride=NB), :] = left
                narrow.append(left.astype(BF16))
            back = nt_dot(inner[f], jnp.concatenate(narrow, axis=1))
            for p in range(devices):
                for h in range(2):
                    at = (2 * p + h) * local_src
                    near[h, PAD + p * local_src : PAD + (p + 1) * local_src, :] = back[at : at + local_src]
            if sweep == 0 and c == 0 and f == 0:
                gather_spans()

            def smooth(g, carry):
                start = pl.multiple_of(g * block, 8)
                rows_of = pl.ds(start, block)
                span, share = spans[rows_of, span_lanes], shares[rows_of, span_lanes]
                pair = []
                for h in range(2):
                    box = near[h, pl.ds(start + PAD, block), :]
                    smoothed = box
                    for offset in range(1, RADIUS + 1):
                        box = box + (
                            near[h, pl.ds(start + PAD + offset, block), :]
                            + near[h, pl.ds(start + PAD - offset, block), :]
                        )
                        smoothed = jnp.where(span >= offset, box, smoothed)
                    pair.append(smoothed * share)
                for n in range(per):
                    slab = jnp.concatenate([half[n * local_src : (n + 1) * local_src] for half in pair], axis=0)
                    part = slice(f * 2 * local_src, (f + 1) * 2 * local_src)
                    back_slabs[sweep * chunks + c, g * per + n, part, :] = slab.astype(BF16)
                return carry

            lax.fori_loop(0, devices // per, smooth, 0, unroll=4)
        exchange(2 * sweep + 1, c, back_slabs, edge_slabs)

    def gather_spans():
        if side > 1:
            await_radii(1, radii_recv)
        for p in range(devices):
            at = p * local_src
            span = radii[p % side, p // side].astype(F32)
            spans[at : at + local_src, :] = span
            shares[at : at + local_src, :] = 1.0 / (2.0 * span + 1.0)

    def trace_side(sweep, c):
        place = sweep * chunks + c
        await_all(2 * sweep + 1, c, edge_slabs, recv_sem)
        if sweep == 1 and c == chunks - 1:
            last_ref[...] = edge_slabs[place]
            return
        flat[...] = edge_slabs[place].astype(F32).reshape(rows * local_src, width)
        lanes = pl.ds(c * width, width)

        def source(g, carry):
            updates = []
            for n in range(pack):
                s = g * pack + n
                spectrum = flat[pl.ds(s, rows, stride=local_src), :].astype(BF16)
                step = tn_dot(jnp.concatenate([spectrum, spectrum], axis=0), synthesis_ref[...])
                if sweep == 0:
                    update = soft(field[c, s].astype(F32) + step)
                    field_ref[s, lanes, :] = update
                    updates.append(update.astype(BF16))
                else:
                    field_ref[s, lanes, :] = soft(field_ref[s, lanes, :] + step)
            if sweep == 0:
                analyse(g * pack, jnp.concatenate(updates, axis=0))
            return carry

        lax.fori_loop(0, local_src // pack, source, 0, unroll=4 // pack)
        if sweep == 0:
            ship(1, c)

    tables[0].wait()
    for c in range(chunks):
        load(c).wait()

        def source(g, carry):
            analyse(g * pack, field[c, pl.ds(g * pack, pack)].reshape(pack * width, samples))
            return carry

        lax.fori_loop(0, local_src // pack, source, 0, unroll=4 // pack)
        if c == chunks - 1:
            if planes > 1:
                await_radii(0, radii_recv)
            for step in range(1, side):
                radii_around(step).start()
        ship(0, c)
    for n, table in enumerate(tables):
        if n not in (0, 3):
            table.wait()
    build_operator(block_ref, multiples_ref, inner, local_src)
    for h in range(2):
        near[h, 0:PAD, :] = jnp.zeros((PAD, width), F32)
        near[h, PAD + devices * local_src :, :] = jnp.zeros((PAD, width), F32)
    for sweep in range(2):
        for c in range(chunks):
            own(sweep, c)
        for c in range(chunks):
            trace_side(sweep, c)
    for phase in range(4):
        for c in range(chunks):
            await_all(phase, c, back_slabs if phase % 2 else out_slabs, send_sem)
    if planes > 1:
        await_radii(0, radii_send)
    if side > 1:
        await_radii(1, radii_send)


def finish_kernel(
    once_ref, last_ref, residual_ref, synthesis_hbm, field_hbm, residual_hbm,
    done, flat, synthesis_ref, ready_sem, done_sem, residual_sem, table_sem,
):
    local_src, receivers, _ = once_ref.shape
    width = last_ref.shape[2]
    rows = flat.shape[0] // local_src
    start = receivers - width
    ready = pltpu.make_async_copy(once_ref.at[:, pl.ds(0, start), :], field_hbm.at[:, pl.ds(0, start), :], ready_sem)
    residual = pltpu.make_async_copy(residual_ref, residual_hbm, residual_sem)
    table = pltpu.make_async_copy(synthesis_hbm, synthesis_ref, table_sem)
    table.start()
    if start:

        def early(s, carry):
            pltpu.make_async_copy(
                once_ref.at[s, pl.ds(0, start), :], field_hbm.at[s, pl.ds(0, start), :], ready_sem
            ).start()
            return carry

        lax.fori_loop(0, local_src, early, 0)
    residual.start()
    flat[...] = last_ref[...].astype(F32).reshape(flat.shape)
    table.wait()

    def source(s, carry):
        spectrum = flat[pl.ds(s, rows, stride=local_src), :].astype(BF16)
        step = tn_dot(jnp.concatenate([spectrum, spectrum], axis=0), synthesis_ref[...])
        done[s] = soft(once_ref[s, pl.ds(start, width), :] + step)
        pltpu.make_async_copy(done.at[s], field_hbm.at[s, pl.ds(start, width), :], done_sem).start()
        return carry

    lax.fori_loop(0, local_src, source, 0, unroll=4)
    pltpu.make_async_copy(done, field_hbm.at[:, pl.ds(start, width), :], done_sem).wait()
    residual.wait()
    if start:
        ready.wait()


def on_device(devices, start_field, recorded, multiples, block_index, radius):
    local_src, receivers, samples = start_field.shape
    local_freq = recorded.shape[0]
    rows = 2 * local_freq * devices
    width = 128
    chunks = receivers // width
    table = dft_table(local_freq * devices, samples)
    analysis = jnp.concatenate(halves(table.T), axis=0)
    high, low = halves(step_size * table.T)
    synthesis = jnp.concatenate([high, low], axis=0)
    side = math.gcd(devices, 8)
    sources = devices * local_src
    vmem = pl.BlockSpec(memory_space=pltpu.VMEM)
    hbm = pl.BlockSpec(memory_space=pltpu.HBM)
    slab = pltpu.VMEM((2 * chunks, devices, local_freq * 2 * local_src, width), BF16)
    flat = pltpu.VMEM((rows * local_src, width), F32)
    field_shape = jax.ShapeDtypeStruct(start_field.shape, F32)
    residual_shape = jax.ShapeDtypeStruct((local_freq, receivers * NB, 2 * BS), F32)
    once, last, residual = pl.pallas_call(
        functools.partial(sweeps_kernel, devices, chunks, width),
        out_shape=(field_shape, jax.ShapeDtypeStruct((devices, local_freq * 2 * local_src, width), BF16), residual_shape),
        in_specs=[hbm] * 7,
        out_specs=(vmem, vmem, vmem),
        scratch_shapes=[
            pltpu.VMEM((chunks, local_src, width, samples), BF16),
            flat,
            flat,
            pltpu.VMEM((2, sources + 2 * PAD, width), F32),
            pltpu.VMEM((side, devices // side, local_src, receivers), BF16),
            pltpu.VMEM((sources, receivers), F32),
            pltpu.VMEM((sources, receivers), F32),
            pltpu.VMEM((width * NB, 2 * BS), F32),
            pltpu.VMEM((local_freq, devices * 2 * local_src, NB * 2 * BS), BF16),
            slab,
            slab,
            slab,
            slab,
            pltpu.SMEM(block_index.shape, block_index.dtype),
            pltpu.VMEM((local_freq, receivers * NB, 2 * BS), BF16),
            pltpu.VMEM(multiples.shape, BF16),
            pltpu.VMEM(radius.shape, radius.dtype),
            pltpu.VMEM(analysis.shape, BF16),
            pltpu.VMEM(synthesis.shape, BF16),
            pltpu.SemaphoreType.DMA((chunks,)),
            pltpu.SemaphoreType.DMA((4 * chunks,)),
            pltpu.SemaphoreType.DMA((4 * chunks,)),
            pltpu.SemaphoreType.DMA((6,)),
            pltpu.SemaphoreType.DMA((2,)),
            pltpu.SemaphoreType.DMA((2,)),
        ],
        compiler_params=pltpu.CompilerParams(
            collective_id=0, has_side_effects=True, vmem_limit_bytes=28 << 20
        ),
    )(
        *(
            pltpu.with_memory_space_constraint(value, pltpu.HBM)
            for value in (
                block_index, start_field, recorded.reshape(local_freq, receivers * NB, 2 * BS), multiples, radius,
                analysis, synthesis,
            )
        )
    )
    field, residual = pl.pallas_call(
        finish_kernel,
        out_shape=(field_shape, residual_shape),
        in_specs=[vmem] * 3 + [hbm],
        out_specs=(hbm, hbm),
        scratch_shapes=[
            pltpu.VMEM((local_src, width, samples), F32),
            flat,
            pltpu.VMEM(synthesis.shape, BF16),
            pltpu.SemaphoreType.DMA,
            pltpu.SemaphoreType.DMA,
            pltpu.SemaphoreType.DMA,
            pltpu.SemaphoreType.DMA,
        ],
        compiler_params=pltpu.CompilerParams(vmem_limit_bytes=12 << 20),
    )(once, last, residual, pltpu.with_memory_space_constraint(synthesis, pltpu.HBM))
    return field, residual.reshape(recorded.shape)


def solution(mesh):
    placed = (
        P(("grp", "freq"), None, None),
        P(("grp", "freq"), None, None, None),
        P(("grp", "freq"), None, None, None, None),
        P(),
        P(("grp", "freq"), None),
    )
    return jax.shard_map(
        functools.partial(on_device, mesh.shape["freq"]),
        mesh=mesh,
        in_specs=placed,
        out_specs=(P(("grp", "freq"), None, None), P(("grp", "freq"), None, None, None)),
        check_vma=False,
    )
```

```python
import functools
import math

import jax
import jax.numpy as jnp
import numpy as np
from jax import lax
from jax.experimental import pallas as pl
from jax.experimental.pallas import tpu as pltpu
from jax.sharding import PartitionSpec as P

NB = 4
BS = 64
BANDS = 3
RADIUS = 4
PAD = 8

step_size = 0.5
shrinkage = 0.05

BF16 = jnp.bfloat16
F32 = jnp.float32


def dft_table(freq_count, samples):
    phases = (np.arange(samples)[:, None] * (np.arange(freq_count) + 1)[None, :]) % samples
    angles = phases.astype(np.float64) * (2.0 * math.pi / samples)
    stacked = np.stack([np.cos(angles), -np.sin(angles)], axis=-1)
    return (stacked.reshape(samples, 2 * freq_count) / math.sqrt(samples)).astype(np.float32)


def halves(table):
    high = jnp.asarray(table).astype(BF16)
    low = (jnp.asarray(table) - high.astype(F32)).astype(BF16)
    return high, low


def soft(update):
    return update - jnp.clip(update, -shrinkage, shrinkage)


def nt_dot(a, b):
    return lax.dot_general(a, b, (((1,), (1,)), ((), ())), preferred_element_type=F32)


def tn_dot(a, b):
    return lax.dot_general(a, b, (((0,), (0,)), ((), ())), preferred_element_type=F32)


def build_operator(block_ref, multiples_ref, inner, local_src):
    parts = BS // local_src
    for f in range(multiples_ref.shape[0]):
        for j in range(NB):
            terms = [multiples_ref[f, j, b].astype(F32) for b in range(BANDS)]
            for m in range(NB):
                block = None
                for b in range(BANDS):
                    term = terms[b] * jnp.where(block_ref[j, b] == m, 1.0, 0.0)
                    block = term if block is None else block + term
                turned = jnp.concatenate([-block[:, BS:], block[:, :BS]], axis=1)
                for q in range(parts):
                    for c, half in enumerate((block, turned)):
                        row = ((m * parts + q) * 2 + c) * local_src
                        piece = half[q * local_src : (q + 1) * local_src]
                        inner[f, row : row + local_src, j * 2 * BS : (j + 1) * 2 * BS] = piece.astype(BF16)


def sweeps_kernel(
    devices, chunks, width,
    block_hbm, start_hbm, recorded_hbm, multiples_hbm, radius_hbm, analysis_hbm, synthesis_hbm,
    field_ref, last_ref, residual_ref,
    field, wide, flat, near, radii, spans, shares, given, inner, out_slabs, in_slabs, back_slabs, edge_slabs,
    block_ref, recorded_ref, multiples_ref, radius_ref, analysis_ref, synthesis_ref,
    load_sem, send_sem, recv_sem, table_sem, radii_send, radii_recv,
):
    me = lax.axis_index("freq")
    local_src, _, samples = start_hbm.shape
    local_freq = multiples_hbm.shape[0]
    rows = analysis_ref.shape[0] // 2
    per = max(1, 8 // local_src)
    block = per * local_src
    block_cols = 2 * BS

    def load(c):
        return pltpu.make_async_copy(start_hbm.at[:, pl.ds(c * width, width), :], field.at[c], load_sem.at[c])

    load(0).start()
    tables = [
        pltpu.make_async_copy(source, target, table_sem.at[n])
        for n, (source, target) in enumerate(
            (
                (analysis_hbm, analysis_ref),
                (block_hbm, block_ref),
                (multiples_hbm, multiples_ref),
                (radius_hbm, radius_ref),
                (recorded_hbm, recorded_ref),
                (synthesis_hbm, synthesis_ref),
            )
        )
    ]
    tables[0].start()
    for c in range(1, chunks):
        load(c).start()
    for table in tables[1:]:
        table.start()
    barrier = pltpu.get_barrier_semaphore()
    for shift in range(1, devices):
        pl.semaphore_signal(
            barrier, inc=1, device_id={"freq": lax.rem(me + shift, devices)}, device_id_type=pl.DeviceIdType.MESH
        )

    def exchange(phase, c, sources, targets):
        slot = phase * chunks + c
        place = (phase // 2) * chunks + c

        def send(step, carry):
            peer = step + (step >= me).astype(jnp.int32)
            pltpu.make_async_remote_copy(
                src_ref=sources.at[place, peer],
                dst_ref=targets.at[place, me],
                send_sem=send_sem.at[phase % 2],
                recv_sem=recv_sem.at[slot],
                device_id={"freq": peer},
                device_id_type=pl.DeviceIdType.MESH,
            ).start()
            return carry

        lax.fori_loop(0, devices - 1, send, 0)
        targets[place, me] = sources[place, me]

    def await_all(phase, c, refs):
        whole = refs.at[(phase // 2) * chunks + c, pl.ds(0, devices - 1)]
        pltpu.make_async_copy(whole, whole, recv_sem.at[phase * chunks + c]).wait()

    side = radii.shape[1]
    planes = devices // side
    plane, spot = me // side, lax.rem(me, side)

    def radii_across(step):
        return pltpu.make_async_remote_copy(
            src_ref=radii.at[:, spot, plane],
            dst_ref=radii.at[:, spot, plane],
            send_sem=radii_send.at[0],
            recv_sem=radii_recv.at[chunks],
            device_id={"freq": lax.rem(plane + step, planes) * side + spot},
            device_id_type=pl.DeviceIdType.MESH,
        )

    def radii_around(c, step):
        return pltpu.make_async_remote_copy(
            src_ref=radii.at[c, spot],
            dst_ref=radii.at[c, spot],
            send_sem=radii_send.at[1],
            recv_sem=radii_recv.at[c],
            device_id={"freq": plane * side + lax.rem(spot + step, side)},
            device_id_type=pl.DeviceIdType.MESH,
        )

    def await_across(sem):
        if planes > 1:
            several = radii.at[:, 0, pl.ds(0, planes - 1)]
            pltpu.make_async_copy(several, several, sem).wait()

    def pass_around(c):
        for step in range(1, side):
            radii_around(c, step).start()

    pack = math.gcd(local_src, 2)

    def analyse(s, samples):
        both = nt_dot(analysis_ref[...], samples)
        both = both[:rows] + both[rows:]
        for n in range(pack):
            wide[pl.ds(s + n, rows, stride=local_src), :] = both[:, n * width : (n + 1) * width]

    def ship(sweep, c):
        slabs = wide[...].reshape(devices, local_freq * 2 * local_src, width)
        out_slabs[sweep * chunks + c] = slabs.astype(BF16)
        if sweep == 0 and c == 0:
            tables[3].wait()
            mine = radius_ref[...].astype(F32).astype(BF16)
            for n in range(chunks):
                radii[n, spot, plane] = mine[:, n * width : (n + 1) * width]
            pl.semaphore_wait(barrier, devices - 1)
            for step in range(1, planes):
                radii_across(step).start()
        exchange(2 * sweep, c, out_slabs, in_slabs)

    def own(sweep, c):
        await_all(2 * sweep, c, in_slabs)
        arrived = in_slabs[sweep * chunks + c].astype(F32)
        span_lanes = pl.ds(c * width, width)
        for f in range(local_freq):
            part = arrived[:, f * 2 * local_src : (f + 1) * 2 * local_src]
            owned = part.reshape(devices * 2 * local_src, width).T.astype(BF16)
            predicted = jnp.dot(owned, inner[f], preferred_element_type=F32)
            given[...] = recorded_ref[f, pl.ds(c * width * NB, width * NB), :].astype(F32)
            narrow = []
            for j in range(NB):
                left = given[pl.ds(j, width, stride=NB), :] - predicted[:, j * block_cols : (j + 1) * block_cols]
                if sweep == 1:
                    residual_ref[f, pl.ds(c * width * NB + j, width, stride=NB), :] = left
                narrow.append(left.astype(BF16))
            back = nt_dot(inner[f], jnp.concatenate(narrow, axis=1))
            for p in range(devices):
                for h in range(2):
                    at = (2 * p + h) * local_src
                    near[h, PAD + p * local_src : PAD + (p + 1) * local_src, :] = back[at : at + local_src]
            if sweep == 0 and f == 0:
                gather_spans(c)

            def smooth(g, carry):
                start = pl.multiple_of(g * block, 8)
                rows_of = pl.ds(start, block)
                span, share = spans[rows_of, span_lanes], shares[rows_of, span_lanes]
                pair = []
                for h in range(2):
                    box = near[h, pl.ds(start + PAD, block), :]
                    smoothed = box
                    for offset in range(1, RADIUS + 1):
                        box = box + (
                            near[h, pl.ds(start + PAD + offset, block), :]
                            + near[h, pl.ds(start + PAD - offset, block), :]
                        )
                        smoothed = jnp.where(span >= offset, box, smoothed)
                    pair.append(smoothed * share)
                for n in range(per):
                    slab = jnp.concatenate([half[n * local_src : (n + 1) * local_src] for half in pair], axis=0)
                    part = slice(f * 2 * local_src, (f + 1) * 2 * local_src)
                    back_slabs[sweep * chunks + c, g * per + n, part, :] = slab.astype(BF16)
                return carry

            lax.fori_loop(0, devices // per, smooth, 0, unroll=4)
        exchange(2 * sweep + 1, c, back_slabs, edge_slabs)
        if sweep == 0 and c + 2 < chunks:
            pass_around(c + 2)

    def gather_spans(c):
        if side > 1:
            several = radii.at[c, pl.ds(0, side - 1)]
            pltpu.make_async_copy(several, several, radii_recv.at[c]).wait()
        for p in range(devices):
            at = p * local_src
            span = radii[c, p % side, p // side].astype(F32)
            spans[at : at + local_src, c * width : (c + 1) * width] = span
            shares[at : at + local_src, c * width : (c + 1) * width] = 1.0 / (2.0 * span + 1.0)

    def trace_side(sweep, c):
        place = sweep * chunks + c
        await_all(2 * sweep + 1, c, edge_slabs)
        if sweep == 1 and c == chunks - 1:
            last_ref[...] = edge_slabs[place]
            return
        flat[...] = edge_slabs[place].astype(F32).reshape(rows * local_src, width)
        lanes = pl.ds(c * width, width)

        def source(g, carry):
            updates = []
            for n in range(pack):
                s = g * pack + n
                spectrum = flat[pl.ds(s, rows, stride=local_src), :].astype(BF16)
                step = tn_dot(jnp.concatenate([spectrum, spectrum], axis=0), synthesis_ref[...])
                if sweep == 0:
                    update = soft(field[c, s].astype(F32) + step)
                    field_ref[s, lanes, :] = update
                    updates.append(update.astype(BF16))
                else:
                    field_ref[s, lanes, :] = soft(field_ref[s, lanes, :] + step)
            if sweep == 0:
                analyse(g * pack, jnp.concatenate(updates, axis=0))
            return carry

        lax.fori_loop(0, local_src // pack, source, 0, unroll=4 // pack)
        if sweep == 0:
            ship(1, c)

    tables[0].wait()
    for c in range(chunks):
        load(c).wait()

        def source(g, carry):
            analyse(g * pack, field[c, pl.ds(g * pack, pack)].reshape(pack * width, samples))
            return carry

        lax.fori_loop(0, local_src // pack, source, 0, unroll=4 // pack)
        if c == min(1, chunks - 1):
            await_across(radii_recv.at[chunks])
        if c == min(1, chunks - 1):
            pass_around(0)
        ship(0, c)
    if chunks > 1:
        pass_around(1)
    for n, table in enumerate(tables):
        if n not in (0, 3):
            table.wait()
    build_operator(block_ref, multiples_ref, inner, local_src)
    for h in range(2):
        near[h, 0:PAD, :] = jnp.zeros((PAD, width), F32)
        near[h, PAD + devices * local_src :, :] = jnp.zeros((PAD, width), F32)
    for sweep in range(2):
        for c in range(chunks):
            own(sweep, c)
        for c in range(chunks):
            trace_side(sweep, c)
    for n, slabs in enumerate((out_slabs, back_slabs)):
        sent = slabs.at[:, pl.ds(0, devices - 1)]
        pltpu.make_async_copy(sent, sent, send_sem.at[n]).wait()
    await_across(radii_send.at[0])
    if side > 1:
        sent = radii.at[:, pl.ds(0, side - 1)]
        pltpu.make_async_copy(sent, sent, radii_send.at[1]).wait()


def finish_kernel(
    once_ref, last_ref, residual_ref, synthesis_hbm, field_hbm, residual_hbm,
    done, flat, synthesis_ref, ready_sem, done_sem, residual_sem, table_sem,
):
    local_src, receivers, _ = once_ref.shape
    width = last_ref.shape[2]
    rows = flat.shape[0] // local_src
    start = receivers - width
    ready = pltpu.make_async_copy(once_ref.at[:, pl.ds(0, start), :], field_hbm.at[:, pl.ds(0, start), :], ready_sem)
    residual = pltpu.make_async_copy(residual_ref, residual_hbm, residual_sem)
    table = pltpu.make_async_copy(synthesis_hbm, synthesis_ref, table_sem)
    table.start()
    if start:

        def early(s, carry):
            pltpu.make_async_copy(
                once_ref.at[s, pl.ds(0, start), :], field_hbm.at[s, pl.ds(0, start), :], ready_sem
            ).start()
            return carry

        lax.fori_loop(0, local_src, early, 0)
    residual.start()
    flat[...] = last_ref[...].astype(F32).reshape(flat.shape)
    table.wait()

    def source(s, carry):
        spectrum = flat[pl.ds(s, rows, stride=local_src), :].astype(BF16)
        step = tn_dot(jnp.concatenate([spectrum, spectrum], axis=0), synthesis_ref[...])
        done[s] = soft(once_ref[s, pl.ds(start, width), :] + step)
        pltpu.make_async_copy(done.at[s], field_hbm.at[s, pl.ds(start, width), :], done_sem).start()
        return carry

    lax.fori_loop(0, local_src, source, 0, unroll=4)
    pltpu.make_async_copy(done, field_hbm.at[:, pl.ds(start, width), :], done_sem).wait()
    residual.wait()
    if start:
        ready.wait()


def on_device(devices, start_field, recorded, multiples, block_index, radius):
    local_src, receivers, samples = start_field.shape
    local_freq = recorded.shape[0]
    rows = 2 * local_freq * devices
    width = 128
    chunks = receivers // width
    table = dft_table(local_freq * devices, samples)
    analysis = jnp.concatenate(halves(table.T), axis=0)
    high, low = halves(step_size * table.T)
    synthesis = jnp.concatenate([high, low], axis=0)
    side = math.gcd(devices, 8)
    sources = devices * local_src
    vmem = pl.BlockSpec(memory_space=pltpu.VMEM)
    hbm = pl.BlockSpec(memory_space=pltpu.HBM)
    slab = pltpu.VMEM((2 * chunks, devices, local_freq * 2 * local_src, width), BF16)
    flat = pltpu.VMEM((rows * local_src, width), F32)
    field_shape = jax.ShapeDtypeStruct(start_field.shape, F32)
    residual_shape = jax.ShapeDtypeStruct((local_freq, receivers * NB, 2 * BS), F32)
    once, last, residual = pl.pallas_call(
        functools.partial(sweeps_kernel, devices, chunks, width),
        out_shape=(field_shape, jax.ShapeDtypeStruct((devices, local_freq * 2 * local_src, width), BF16), residual_shape),
        in_specs=[hbm] * 7,
        out_specs=(vmem, vmem, vmem),
        scratch_shapes=[
            pltpu.VMEM((chunks, local_src, width, samples), BF16),
            flat,
            flat,
            pltpu.VMEM((2, sources + 2 * PAD, width), F32),
            pltpu.VMEM((chunks, side, devices // side, local_src, width), BF16),
            pltpu.VMEM((sources, receivers), F32),
            pltpu.VMEM((sources, receivers), F32),
            pltpu.VMEM((width * NB, 2 * BS), F32),
            pltpu.VMEM((local_freq, devices * 2 * local_src, NB * 2 * BS), BF16),
            slab,
            slab,
            slab,
            slab,
            pltpu.SMEM(block_index.shape, block_index.dtype),
            pltpu.VMEM((local_freq, receivers * NB, 2 * BS), BF16),
            pltpu.VMEM(multiples.shape, BF16),
            pltpu.VMEM(radius.shape, radius.dtype),
            pltpu.VMEM(analysis.shape, BF16),
            pltpu.VMEM(synthesis.shape, BF16),
            pltpu.SemaphoreType.DMA((chunks,)),
            pltpu.SemaphoreType.DMA((2,)),
            pltpu.SemaphoreType.DMA((4 * chunks,)),
            pltpu.SemaphoreType.DMA((6,)),
            pltpu.SemaphoreType.DMA((2,)),
            pltpu.SemaphoreType.DMA((chunks + 1,)),
        ],
        compiler_params=pltpu.CompilerParams(
            collective_id=0, has_side_effects=True, vmem_limit_bytes=28 << 20
        ),
    )(
        *(
            pltpu.with_memory_space_constraint(value, pltpu.HBM)
            for value in (
                block_index, start_field, recorded.reshape(local_freq, receivers * NB, 2 * BS), multiples, radius,
                analysis, synthesis,
            )
        )
    )
    field, residual = pl.pallas_call(
        finish_kernel,
        out_shape=(field_shape, residual_shape),
        in_specs=[vmem] * 3 + [hbm],
        out_specs=(hbm, hbm),
        scratch_shapes=[
            pltpu.VMEM((local_src, width, samples), F32),
            flat,
            pltpu.VMEM(synthesis.shape, BF16),
            pltpu.SemaphoreType.DMA,
            pltpu.SemaphoreType.DMA,
            pltpu.SemaphoreType.DMA,
            pltpu.SemaphoreType.DMA,
        ],
        compiler_params=pltpu.CompilerParams(vmem_limit_bytes=12 << 20),
    )(once, last, residual, pltpu.with_memory_space_constraint(synthesis, pltpu.HBM))
    return field, residual.reshape(recorded.shape)


def solution(mesh):
    placed = (
        P(("grp", "freq"), None, None),
        P(("grp", "freq"), None, None, None),
        P(("grp", "freq"), None, None, None, None),
        P(),
        P(("grp", "freq"), None),
    )
    return jax.shard_map(
        functools.partial(on_device, mesh.shape["freq"]),
        mesh=mesh,
        in_specs=placed,
        out_specs=(P(("grp", "freq"), None, None), P(("grp", "freq"), None, None, None)),
        check_vma=False,
    )
```

```python
import functools
import math

import jax
import jax.numpy as jnp
import numpy as np
from jax import lax
from jax.experimental import pallas as pl
from jax.experimental.pallas import tpu as pltpu
from jax.sharding import PartitionSpec as P

NB = 4
BS = 64
BANDS = 3
RADIUS = 4
PAD = 8

step_size = 0.5
shrinkage = 0.05

BF16 = jnp.bfloat16
F32 = jnp.float32


def dft_table(freq_count, samples):
    phases = (np.arange(samples)[:, None] * (np.arange(freq_count) + 1)[None, :]) % samples
    angles = phases.astype(np.float64) * (2.0 * math.pi / samples)
    stacked = np.stack([np.cos(angles), -np.sin(angles)], axis=-1)
    return (stacked.reshape(samples, 2 * freq_count) / math.sqrt(samples)).astype(np.float32)


def halves(table):
    high = jnp.asarray(table).astype(BF16)
    low = (jnp.asarray(table) - high.astype(F32)).astype(BF16)
    return high, low


def soft(update):
    return update - jnp.clip(update, -shrinkage, shrinkage)


def nt_dot(a, b):
    return lax.dot_general(a, b, (((1,), (1,)), ((), ())), preferred_element_type=F32)


def tn_dot(a, b):
    return lax.dot_general(a, b, (((0,), (0,)), ((), ())), preferred_element_type=F32)


def build_operator(block_ref, multiples_ref, inner, local_src):
    parts = BS // local_src
    for f in range(multiples_ref.shape[0]):
        for j in range(NB):
            terms = [multiples_ref[f, j, b].astype(F32) for b in range(BANDS)]
            for m in range(NB):
                block = None
                for b in range(BANDS):
                    term = terms[b] * jnp.where(block_ref[j, b] == m, 1.0, 0.0)
                    block = term if block is None else block + term
                turned = jnp.concatenate([-block[:, BS:], block[:, :BS]], axis=1)
                for q in range(parts):
                    for c, half in enumerate((block, turned)):
                        row = ((m * parts + q) * 2 + c) * local_src
                        piece = half[q * local_src : (q + 1) * local_src]
                        inner[f, row : row + local_src, j * 2 * BS : (j + 1) * 2 * BS] = piece.astype(BF16)


def sweeps_kernel(
    devices, chunks, width,
    block_hbm, start_hbm, recorded_hbm, multiples_hbm, radius_hbm, analysis_hbm, synthesis_hbm,
    field_ref, last_ref, residual_ref,
    field, wide, flat, near, radii, spans, shares, given, inner, out_slabs, in_slabs, back_slabs, edge_slabs,
    block_ref, recorded_ref, multiples_ref, radius_ref, analysis_ref, synthesis_ref,
    load_sem, send_sem, recv_sem, table_sem, radii_send, radii_recv,
):
    me = lax.axis_index("freq")
    local_src, _, samples = start_hbm.shape
    local_freq = multiples_hbm.shape[0]
    rows = analysis_ref.shape[0] // 2
    per = max(1, 8 // local_src)
    block = per * local_src
    block_cols = 2 * BS

    def load(c):
        return pltpu.make_async_copy(start_hbm.at[:, pl.ds(c * width, width), :], field.at[c], load_sem.at[c])

    barrier = pltpu.get_barrier_semaphore()
    for shift in range(1, devices):
        pl.semaphore_signal(
            barrier, inc=1, device_id={"freq": lax.rem(me + shift, devices)}, device_id_type=pl.DeviceIdType.MESH
        )

    load(0).start()
    tables = [
        pltpu.make_async_copy(source, target, table_sem.at[n])
        for n, (source, target) in enumerate(
            (
                (analysis_hbm, analysis_ref),
                (block_hbm, block_ref),
                (multiples_hbm, multiples_ref),
                (radius_hbm, radius_ref),
                (recorded_hbm, recorded_ref),
                (synthesis_hbm, synthesis_ref),
            )
        )
    ]
    tables[0].start()
    for c in range(1, chunks):
        load(c).start()
    for table in tables[1:]:
        table.start()
    def send(phase, c, sources, targets, peer):
        place = (phase // 2) * chunks + c
        return pltpu.make_async_remote_copy(
            src_ref=sources.at[place, peer],
            dst_ref=targets.at[place, me],
            send_sem=send_sem.at[phase % 2],
            recv_sem=recv_sem.at[phase * chunks + c],
            device_id={"freq": peer},
            device_id_type=pl.DeviceIdType.MESH,
        )

    def exchange(phase, c, sources, targets):
        place = (phase // 2) * chunks + c

        def step(n, carry):
            send(phase, c, sources, targets, n + (n >= me).astype(jnp.int32)).start()
            return carry

        lax.fori_loop(0, devices - 1, step, 0)
        targets[place, me] = sources[place, me]

    def await_all(phase, c, refs):
        whole = refs.at[(phase // 2) * chunks + c, pl.ds(0, devices - 1)]
        pltpu.make_async_copy(whole, whole, recv_sem.at[phase * chunks + c]).wait()

    side = radii.shape[1]
    planes = devices // side
    plane, spot = me // side, lax.rem(me, side)

    def radii_across(step):
        return pltpu.make_async_remote_copy(
            src_ref=radii.at[:, spot, plane],
            dst_ref=radii.at[:, spot, plane],
            send_sem=radii_send.at[0],
            recv_sem=radii_recv.at[chunks],
            device_id={"freq": lax.rem(plane + step, planes) * side + spot},
            device_id_type=pl.DeviceIdType.MESH,
        )

    def radii_around(c, step):
        return pltpu.make_async_remote_copy(
            src_ref=radii.at[c, spot],
            dst_ref=radii.at[c, spot],
            send_sem=radii_send.at[1],
            recv_sem=radii_recv.at[c],
            device_id={"freq": plane * side + lax.rem(spot + step, side)},
            device_id_type=pl.DeviceIdType.MESH,
        )

    def await_across(sem):
        if planes > 1:
            several = radii.at[:, 0, pl.ds(0, planes - 1)]
            pltpu.make_async_copy(several, several, sem).wait()

    def pass_around(c):
        for step in range(1, side):
            radii_around(c, step).start()

    pack = math.gcd(local_src, 2)

    def analyse(s, samples):
        both = nt_dot(analysis_ref[...], samples)
        both = both[:rows] + both[rows:]
        for n in range(pack):
            wide[pl.ds(s + n, rows, stride=local_src), :] = both[:, n * width : (n + 1) * width]

    def ship(sweep, c):
        slabs = wide[...].reshape(devices, local_freq * 2 * local_src, width)
        out_slabs[sweep * chunks + c] = slabs.astype(BF16)
        if sweep == 0 and c == 0:
            tables[3].wait()
            mine = radius_ref[...].astype(F32).astype(BF16)
            for n in range(chunks):
                radii[n, spot, plane] = mine[:, n * width : (n + 1) * width]
            pl.semaphore_wait(barrier, devices - 1)
            for step in range(1, planes):
                radii_across(step).start()
        exchange(2 * sweep, c, out_slabs, in_slabs)

    def own(sweep, c):
        await_all(2 * sweep, c, in_slabs)
        arrived = in_slabs[sweep * chunks + c].astype(F32)
        span_lanes = pl.ds(c * width, width)
        for f in range(local_freq):
            part = arrived[:, f * 2 * local_src : (f + 1) * 2 * local_src]
            owned = part.reshape(devices * 2 * local_src, width).T.astype(BF16)
            predicted = jnp.dot(owned, inner[f], preferred_element_type=F32)
            given[...] = recorded_ref[f, pl.ds(c * width * NB, width * NB), :].astype(F32)
            narrow = []
            for j in range(NB):
                left = given[pl.ds(j, width, stride=NB), :] - predicted[:, j * block_cols : (j + 1) * block_cols]
                if sweep == 1:
                    residual_ref[f, pl.ds(c * width * NB + j, width, stride=NB), :] = left
                narrow.append(left.astype(BF16))
            back = nt_dot(inner[f], jnp.concatenate(narrow, axis=1))
            for p in range(devices):
                for h in range(2):
                    at = (2 * p + h) * local_src
                    near[h, PAD + p * local_src : PAD + (p + 1) * local_src, :] = back[at : at + local_src]
            if sweep == 0 and f == 0:
                gather_spans(c)

            def smooth(g, carry):
                start = pl.multiple_of(g * block, 8)
                rows_of = pl.ds(start, block)
                span, share = spans[rows_of, span_lanes], shares[rows_of, span_lanes]
                pair = []
                for h in range(2):
                    box = near[h, pl.ds(start + PAD, block), :]
                    smoothed = box
                    for offset in range(1, RADIUS + 1):
                        box = box + (
                            near[h, pl.ds(start + PAD + offset, block), :]
                            + near[h, pl.ds(start + PAD - offset, block), :]
                        )
                        smoothed = jnp.where(span >= offset, box, smoothed)
                    pair.append(smoothed * share)
                for n in range(per):
                    slab = jnp.concatenate([half[n * local_src : (n + 1) * local_src] for half in pair], axis=0)
                    part = slice(f * 2 * local_src, (f + 1) * 2 * local_src)
                    back_slabs[sweep * chunks + c, g * per + n, part, :] = slab.astype(BF16)
                    if f == local_freq - 1:

                        @pl.when(g * per + n != me)
                        def _():
                            send(2 * sweep + 1, c, back_slabs, edge_slabs, g * per + n).start()

                return carry

            lax.fori_loop(0, devices // per, smooth, 0, unroll=4)
        edge_slabs[sweep * chunks + c, me] = back_slabs[sweep * chunks + c, me]
        if sweep == 0 and c + 2 < chunks:
            pass_around(c + 2)

    def gather_spans(c):
        if side > 1:
            several = radii.at[c, pl.ds(0, side - 1)]
            pltpu.make_async_copy(several, several, radii_recv.at[c]).wait()
        for p in range(devices):
            at = p * local_src
            span = radii[c, p % side, p // side].astype(F32)
            spans[at : at + local_src, c * width : (c + 1) * width] = span
            shares[at : at + local_src, c * width : (c + 1) * width] = 1.0 / (2.0 * span + 1.0)

    def trace_side(sweep, c):
        place = sweep * chunks + c
        await_all(2 * sweep + 1, c, edge_slabs)
        if sweep == 1 and c == chunks - 1:
            last_ref[...] = edge_slabs[place]
            return
        flat[...] = edge_slabs[place].astype(F32).reshape(rows * local_src, width)
        lanes = pl.ds(c * width, width)

        def source(g, carry):
            updates = []
            for n in range(pack):
                s = g * pack + n
                spectrum = flat[pl.ds(s, rows, stride=local_src), :].astype(BF16)
                step = tn_dot(jnp.concatenate([spectrum, spectrum], axis=0), synthesis_ref[...])
                if sweep == 0:
                    update = soft(field[c, s].astype(F32) + step)
                    field_ref[s, lanes, :] = update
                    updates.append(update.astype(BF16))
                else:
                    field_ref[s, lanes, :] = soft(field_ref[s, lanes, :] + step)
            if sweep == 0:
                analyse(g * pack, jnp.concatenate(updates, axis=0))
            return carry

        lax.fori_loop(0, local_src // pack, source, 0, unroll=4 // pack)
        if sweep == 0:
            ship(1, c)

    tables[0].wait()
    for c in range(chunks):
        load(c).wait()

        def source(g, carry):
            analyse(g * pack, field[c, pl.ds(g * pack, pack)].reshape(pack * width, samples))
            return carry

        lax.fori_loop(0, local_src // pack, source, 0, unroll=4 // pack)
        if c == min(1, chunks - 1):
            await_across(radii_recv.at[chunks])
        if c == min(1, chunks - 1):
            pass_around(0)
        ship(0, c)
    if chunks > 1:
        pass_around(1)
    for n, table in enumerate(tables):
        if n not in (0, 3):
            table.wait()
    build_operator(block_ref, multiples_ref, inner, local_src)
    for h in range(2):
        near[h, 0:PAD, :] = jnp.zeros((PAD, width), F32)
        near[h, PAD + devices * local_src :, :] = jnp.zeros((PAD, width), F32)
    for sweep in range(2):
        for c in range(chunks):
            own(sweep, c)
        for c in range(chunks):
            trace_side(sweep, c)
    for n, slabs in enumerate((out_slabs, back_slabs)):
        sent = slabs.at[:, pl.ds(0, devices - 1)]
        pltpu.make_async_copy(sent, sent, send_sem.at[n]).wait()
    await_across(radii_send.at[0])
    if side > 1:
        sent = radii.at[:, pl.ds(0, side - 1)]
        pltpu.make_async_copy(sent, sent, radii_send.at[1]).wait()


def finish_kernel(
    once_ref, last_ref, residual_ref, synthesis_hbm, field_hbm, residual_hbm,
    done, flat, synthesis_ref, ready_sem, done_sem, residual_sem, table_sem,
):
    local_src, receivers, _ = once_ref.shape
    width = last_ref.shape[2]
    rows = flat.shape[0] // local_src
    start = receivers - width
    ready = pltpu.make_async_copy(once_ref.at[:, pl.ds(0, start), :], field_hbm.at[:, pl.ds(0, start), :], ready_sem)
    residual = pltpu.make_async_copy(residual_ref, residual_hbm, residual_sem)
    table = pltpu.make_async_copy(synthesis_hbm, synthesis_ref, table_sem)
    table.start()
    if start:

        def early(s, carry):
            pltpu.make_async_copy(
                once_ref.at[s, pl.ds(0, start), :], field_hbm.at[s, pl.ds(0, start), :], ready_sem
            ).start()
            return carry

        lax.fori_loop(0, local_src, early, 0)
    residual.start()
    flat[...] = last_ref[...].astype(F32).reshape(flat.shape)
    table.wait()

    def source(s, carry):
        spectrum = flat[pl.ds(s, rows, stride=local_src), :].astype(BF16)
        step = tn_dot(jnp.concatenate([spectrum, spectrum], axis=0), synthesis_ref[...])
        done[s] = soft(once_ref[s, pl.ds(start, width), :] + step)
        pltpu.make_async_copy(done.at[s], field_hbm.at[s, pl.ds(start, width), :], done_sem).start()
        return carry

    lax.fori_loop(0, local_src, source, 0, unroll=4)
    pltpu.make_async_copy(done, field_hbm.at[:, pl.ds(start, width), :], done_sem).wait()
    residual.wait()
    if start:
        ready.wait()


def on_device(devices, start_field, recorded, multiples, block_index, radius):
    local_src, receivers, samples = start_field.shape
    local_freq = recorded.shape[0]
    rows = 2 * local_freq * devices
    width = 128
    chunks = receivers // width
    table = dft_table(local_freq * devices, samples)
    analysis = jnp.concatenate(halves(table.T), axis=0)
    high, low = halves(step_size * table.T)
    synthesis = jnp.concatenate([high, low], axis=0)
    side = math.gcd(devices, 8)
    sources = devices * local_src
    vmem = pl.BlockSpec(memory_space=pltpu.VMEM)
    hbm = pl.BlockSpec(memory_space=pltpu.HBM)
    slab = pltpu.VMEM((2 * chunks, devices, local_freq * 2 * local_src, width), BF16)
    flat = pltpu.VMEM((rows * local_src, width), F32)
    field_shape = jax.ShapeDtypeStruct(start_field.shape, F32)
    residual_shape = jax.ShapeDtypeStruct((local_freq, receivers * NB, 2 * BS), F32)
    once, last, residual = pl.pallas_call(
        functools.partial(sweeps_kernel, devices, chunks, width),
        out_shape=(field_shape, jax.ShapeDtypeStruct((devices, local_freq * 2 * local_src, width), BF16), residual_shape),
        in_specs=[hbm] * 7,
        out_specs=(vmem, vmem, vmem),
        scratch_shapes=[
            pltpu.VMEM((chunks, local_src, width, samples), BF16),
            flat,
            flat,
            pltpu.VMEM((2, sources + 2 * PAD, width), F32),
            pltpu.VMEM((chunks, side, devices // side, local_src, width), BF16),
            pltpu.VMEM((sources, receivers), F32),
            pltpu.VMEM((sources, receivers), F32),
            pltpu.VMEM((width * NB, 2 * BS), F32),
            pltpu.VMEM((local_freq, devices * 2 * local_src, NB * 2 * BS), BF16),
            slab,
            slab,
            slab,
            slab,
            pltpu.SMEM(block_index.shape, block_index.dtype),
            pltpu.VMEM((local_freq, receivers * NB, 2 * BS), BF16),
            pltpu.VMEM(multiples.shape, BF16),
            pltpu.VMEM(radius.shape, radius.dtype),
            pltpu.VMEM(analysis.shape, BF16),
            pltpu.VMEM(synthesis.shape, BF16),
            pltpu.SemaphoreType.DMA((chunks,)),
            pltpu.SemaphoreType.DMA((2,)),
            pltpu.SemaphoreType.DMA((4 * chunks,)),
            pltpu.SemaphoreType.DMA((6,)),
            pltpu.SemaphoreType.DMA((2,)),
            pltpu.SemaphoreType.DMA((chunks + 1,)),
        ],
        compiler_params=pltpu.CompilerParams(
            collective_id=0, has_side_effects=True, vmem_limit_bytes=28 << 20
        ),
    )(
        *(
            pltpu.with_memory_space_constraint(value, pltpu.HBM)
            for value in (
                block_index, start_field, recorded.reshape(local_freq, receivers * NB, 2 * BS), multiples, radius,
                analysis, synthesis,
            )
        )
    )
    field, residual = pl.pallas_call(
        finish_kernel,
        out_shape=(field_shape, residual_shape),
        in_specs=[vmem] * 3 + [hbm],
        out_specs=(hbm, hbm),
        scratch_shapes=[
            pltpu.VMEM((local_src, width, samples), F32),
            flat,
            pltpu.VMEM(synthesis.shape, BF16),
            pltpu.SemaphoreType.DMA,
            pltpu.SemaphoreType.DMA,
            pltpu.SemaphoreType.DMA,
            pltpu.SemaphoreType.DMA,
        ],
        compiler_params=pltpu.CompilerParams(vmem_limit_bytes=12 << 20),
    )(once, last, residual, pltpu.with_memory_space_constraint(synthesis, pltpu.HBM))
    return field, residual.reshape(recorded.shape)


def solution(mesh):
    placed = (
        P(("grp", "freq"), None, None),
        P(("grp", "freq"), None, None, None),
        P(("grp", "freq"), None, None, None, None),
        P(),
        P(("grp", "freq"), None),
    )
    return jax.shard_map(
        functools.partial(on_device, mesh.shape["freq"]),
        mesh=mesh,
        in_specs=placed,
        out_specs=(P(("grp", "freq"), None, None), P(("grp", "freq"), None, None, None)),
        check_vma=False,
    )
```

```python
import functools
import math

import jax
import jax.numpy as jnp
import numpy as np
from jax import lax
from jax.experimental import pallas as pl
from jax.experimental.pallas import tpu as pltpu
from jax.sharding import PartitionSpec as P

NB = 4
BS = 64
BANDS = 3
RADIUS = 4
PAD = 8

step_size = 0.5
shrinkage = 0.05

BF16 = jnp.bfloat16
F32 = jnp.float32


def dft_table(freq_count, samples):
    phases = (np.arange(samples)[:, None] * (np.arange(freq_count) + 1)[None, :]) % samples
    angles = phases.astype(np.float64) * (2.0 * math.pi / samples)
    stacked = np.stack([np.cos(angles), -np.sin(angles)], axis=-1)
    return (stacked.reshape(samples, 2 * freq_count) / math.sqrt(samples)).astype(np.float32)


def halves(table):
    high = jnp.asarray(table).astype(BF16)
    low = (jnp.asarray(table) - high.astype(F32)).astype(BF16)
    return high, low


def soft(update):
    return update - jnp.clip(update, -shrinkage, shrinkage)


def nt_dot(a, b):
    return lax.dot_general(a, b, (((1,), (1,)), ((), ())), preferred_element_type=F32)


def tn_dot(a, b):
    return lax.dot_general(a, b, (((0,), (0,)), ((), ())), preferred_element_type=F32)


def build_operator(block_ref, multiples_ref, inner, local_src):
    parts = BS // local_src
    for f in range(multiples_ref.shape[0]):
        for j in range(NB):
            terms = [multiples_ref[f, j, b].astype(F32) for b in range(BANDS)]
            for m in range(NB):
                block = None
                for b in range(BANDS):
                    term = terms[b] * jnp.where(block_ref[j, b] == m, 1.0, 0.0)
                    block = term if block is None else block + term
                turned = jnp.concatenate([-block[:, BS:], block[:, :BS]], axis=1)
                for q in range(parts):
                    for c, half in enumerate((block, turned)):
                        row = ((m * parts + q) * 2 + c) * local_src
                        piece = half[q * local_src : (q + 1) * local_src]
                        inner[f, row : row + local_src, j * 2 * BS : (j + 1) * 2 * BS] = piece.astype(BF16)


def sweeps_kernel(
    devices, chunks, width,
    block_hbm, start_hbm, recorded_hbm, multiples_hbm, radius_hbm, analysis_hbm, synthesis_hbm,
    field_ref, last_ref, residual_ref,
    field, wide, flat, near, radii, spans, shares, given, inner, out_slabs, in_slabs, back_slabs, edge_slabs,
    block_ref, recorded_ref, multiples_ref, radius_ref, analysis_ref, synthesis_ref,
    load_sem, send_sem, recv_sem, table_sem, radii_send, radii_recv,
):
    me = lax.axis_index("freq")
    local_src, _, samples = start_hbm.shape
    local_freq = multiples_hbm.shape[0]
    rows = analysis_ref.shape[0] // 2
    per = max(1, 8 // local_src)
    block = per * local_src
    block_cols = 2 * BS

    def load(c):
        return pltpu.make_async_copy(start_hbm.at[:, pl.ds(c * width, width), :], field.at[c], load_sem.at[c])

    barrier = pltpu.get_barrier_semaphore()
    for shift in range(1, devices):
        pl.semaphore_signal(
            barrier, inc=1, device_id={"freq": lax.rem(me + shift, devices)}, device_id_type=pl.DeviceIdType.MESH
        )

    load(0).start()
    tables = [
        pltpu.make_async_copy(source, target, table_sem.at[n])
        for n, (source, target) in enumerate(
            (
                (analysis_hbm, analysis_ref),
                (block_hbm, block_ref),
                (multiples_hbm, multiples_ref),
                (radius_hbm, radius_ref),
                (recorded_hbm, recorded_ref),
                (synthesis_hbm, synthesis_ref),
            )
        )
    ]
    tables[0].start()
    for c in range(1, chunks):
        load(c).start()
    for table in tables[1:]:
        table.start()
    def exchange(phase, c, sources, targets):
        slot = phase * chunks + c
        place = (phase // 2) * chunks + c

        def send(step, carry):
            peer = step + (step >= me).astype(jnp.int32)
            pltpu.make_async_remote_copy(
                src_ref=sources.at[place, peer],
                dst_ref=targets.at[place, me],
                send_sem=send_sem.at[phase % 2],
                recv_sem=recv_sem.at[slot],
                device_id={"freq": peer},
                device_id_type=pl.DeviceIdType.MESH,
            ).start()
            return carry

        lax.fori_loop(0, devices - 1, send, 0)
        targets[place, me] = sources[place, me]

    def await_all(phase, c, refs):
        whole = refs.at[(phase // 2) * chunks + c, pl.ds(0, devices - 1)]
        pltpu.make_async_copy(whole, whole, recv_sem.at[phase * chunks + c]).wait()

    side = radii.shape[1]
    planes = devices // side
    plane, spot = me // side, lax.rem(me, side)

    def radii_across(part, step):
        lanes = radii.at[0:1] if part == 0 else radii.at[1:]
        return pltpu.make_async_remote_copy(
            src_ref=lanes.at[:, spot, plane],
            dst_ref=lanes.at[:, spot, plane],
            send_sem=radii_send.at[part],
            recv_sem=radii_recv.at[chunks + part],
            device_id={"freq": lax.rem(plane + step, planes) * side + spot},
            device_id_type=pl.DeviceIdType.MESH,
        )

    def radii_around(c, step):
        return pltpu.make_async_remote_copy(
            src_ref=radii.at[c, spot],
            dst_ref=radii.at[c, spot],
            send_sem=radii_send.at[2],
            recv_sem=radii_recv.at[c],
            device_id={"freq": plane * side + lax.rem(spot + step, side)},
            device_id_type=pl.DeviceIdType.MESH,
        )

    def await_across(part, sem):
        if planes > 1 and (part == 0 or chunks > 1):
            several = (radii.at[0:1] if part == 0 else radii.at[1:]).at[:, 0, pl.ds(0, planes - 1)]
            pltpu.make_async_copy(several, several, sem).wait()

    def pass_around(c):
        for step in range(1, side):
            radii_around(c, step).start()

    pack = math.gcd(local_src, 2)

    def analyse(s, samples):
        both = nt_dot(analysis_ref[...], samples)
        both = both[:rows] + both[rows:]
        for n in range(pack):
            wide[pl.ds(s + n, rows, stride=local_src), :] = both[:, n * width : (n + 1) * width]

    def ship(sweep, c):
        slabs = wide[...].reshape(devices, local_freq * 2 * local_src, width)
        out_slabs[sweep * chunks + c] = slabs.astype(BF16)
        if sweep == 0 and c == 0:
            tables[3].wait()
            mine = radius_ref[...].astype(F32).astype(BF16)
            for n in range(chunks):
                radii[n, spot, plane] = mine[:, n * width : (n + 1) * width]
            pl.semaphore_wait(barrier, devices - 1)
            for step in range(1, planes):
                radii_across(0, step).start()
        exchange(2 * sweep, c, out_slabs, in_slabs)
        if sweep == 0 and c == 0 and chunks > 1:
            for step in range(1, planes):
                radii_across(1, step).start()

    def own(sweep, c):
        await_all(2 * sweep, c, in_slabs)
        arrived = in_slabs[sweep * chunks + c].astype(F32)
        span_lanes = pl.ds(c * width, width)
        for f in range(local_freq):
            part = arrived[:, f * 2 * local_src : (f + 1) * 2 * local_src]
            owned = part.reshape(devices * 2 * local_src, width).T.astype(BF16)
            predicted = jnp.dot(owned, inner[f], preferred_element_type=F32)
            given[...] = recorded_ref[f, pl.ds(c * width * NB, width * NB), :].astype(F32)
            narrow = []
            for j in range(NB):
                left = given[pl.ds(j, width, stride=NB), :] - predicted[:, j * block_cols : (j + 1) * block_cols]
                if sweep == 1:
                    residual_ref[f, pl.ds(c * width * NB + j, width, stride=NB), :] = left
                narrow.append(left.astype(BF16))
            back = nt_dot(inner[f], jnp.concatenate(narrow, axis=1))
            for p in range(devices):
                for h in range(2):
                    at = (2 * p + h) * local_src
                    near[h, PAD + p * local_src : PAD + (p + 1) * local_src, :] = back[at : at + local_src]
            if sweep == 0 and f == 0:
                gather_spans(c)

            def smooth(g, carry):
                start = pl.multiple_of(g * block, 8)
                rows_of = pl.ds(start, block)
                span, share = spans[rows_of, span_lanes], shares[rows_of, span_lanes]
                pair = []
                for h in range(2):
                    box = near[h, pl.ds(start + PAD, block), :]
                    smoothed = box
                    for offset in range(1, RADIUS + 1):
                        box = box + (
                            near[h, pl.ds(start + PAD + offset, block), :]
                            + near[h, pl.ds(start + PAD - offset, block), :]
                        )
                        smoothed = jnp.where(span >= offset, box, smoothed)
                    pair.append(smoothed * share)
                for n in range(per):
                    slab = jnp.concatenate([half[n * local_src : (n + 1) * local_src] for half in pair], axis=0)
                    part = slice(f * 2 * local_src, (f + 1) * 2 * local_src)
                    back_slabs[sweep * chunks + c, g * per + n, part, :] = slab.astype(BF16)
                return carry

            lax.fori_loop(0, devices // per, smooth, 0, unroll=4)
        exchange(2 * sweep + 1, c, back_slabs, edge_slabs)
        if sweep == 0 and c + 2 < chunks:
            pass_around(c + 2)

    def gather_spans(c):
        if side > 1:
            several = radii.at[c, pl.ds(0, side - 1)]
            pltpu.make_async_copy(several, several, radii_recv.at[c]).wait()
        for p in range(devices):
            at = p * local_src
            span = radii[c, p % side, p // side].astype(F32)
            spans[at : at + local_src, c * width : (c + 1) * width] = span
            shares[at : at + local_src, c * width : (c + 1) * width] = 1.0 / (2.0 * span + 1.0)

    def trace_side(sweep, c):
        place = sweep * chunks + c
        await_all(2 * sweep + 1, c, edge_slabs)
        if sweep == 1 and c == chunks - 1:
            last_ref[...] = edge_slabs[place]
            return
        flat[...] = edge_slabs[place].astype(F32).reshape(rows * local_src, width)
        lanes = pl.ds(c * width, width)

        def source(g, carry):
            updates = []
            for n in range(pack):
                s = g * pack + n
                spectrum = flat[pl.ds(s, rows, stride=local_src), :].astype(BF16)
                step = tn_dot(jnp.concatenate([spectrum, spectrum], axis=0), synthesis_ref[...])
                if sweep == 0:
                    update = soft(field[c, s].astype(F32) + step)
                    field_ref[s, lanes, :] = update
                    updates.append(update.astype(BF16))
                else:
                    field_ref[s, lanes, :] = soft(field_ref[s, lanes, :] + step)
            if sweep == 0:
                analyse(g * pack, jnp.concatenate(updates, axis=0))
            return carry

        lax.fori_loop(0, local_src // pack, source, 0, unroll=4 // pack)
        if sweep == 0:
            ship(1, c)

    tables[0].wait()
    for c in range(chunks):
        load(c).wait()

        def source(g, carry):
            analyse(g * pack, field[c, pl.ds(g * pack, pack)].reshape(pack * width, samples))
            return carry

        lax.fori_loop(0, local_src // pack, source, 0, unroll=4 // pack)
        if c == min(1, chunks - 1):
            await_across(0, radii_recv.at[chunks])
        if c == min(1, chunks - 1):
            pass_around(0)
        ship(0, c)
    await_across(1, radii_recv.at[chunks + 1])
    if chunks > 1:
        pass_around(1)
    for n, table in enumerate(tables):
        if n not in (0, 3):
            table.wait()
    build_operator(block_ref, multiples_ref, inner, local_src)
    for h in range(2):
        near[h, 0:PAD, :] = jnp.zeros((PAD, width), F32)
        near[h, PAD + devices * local_src :, :] = jnp.zeros((PAD, width), F32)
    for sweep in range(2):
        for c in range(chunks):
            own(sweep, c)
        for c in range(chunks):
            trace_side(sweep, c)
    for n, slabs in enumerate((out_slabs, back_slabs)):
        sent = slabs.at[:, pl.ds(0, devices - 1)]
        pltpu.make_async_copy(sent, sent, send_sem.at[n]).wait()
    await_across(0, radii_send.at[0])
    await_across(1, radii_send.at[1])
    if side > 1:
        sent = radii.at[:, pl.ds(0, side - 1)]
        pltpu.make_async_copy(sent, sent, radii_send.at[2]).wait()


def finish_kernel(
    once_ref, last_ref, residual_ref, synthesis_hbm, field_hbm, residual_hbm,
    done, flat, synthesis_ref, ready_sem, done_sem, residual_sem, table_sem,
):
    local_src, receivers, _ = once_ref.shape
    width = last_ref.shape[2]
    rows = flat.shape[0] // local_src
    start = receivers - width
    ready = pltpu.make_async_copy(once_ref.at[:, pl.ds(0, start), :], field_hbm.at[:, pl.ds(0, start), :], ready_sem)
    residual = pltpu.make_async_copy(residual_ref, residual_hbm, residual_sem)
    table = pltpu.make_async_copy(synthesis_hbm, synthesis_ref, table_sem)
    table.start()
    if start:

        def early(s, carry):
            pltpu.make_async_copy(
                once_ref.at[s, pl.ds(0, start), :], field_hbm.at[s, pl.ds(0, start), :], ready_sem
            ).start()
            return carry

        lax.fori_loop(0, local_src, early, 0)
    residual.start()
    flat[...] = last_ref[...].astype(F32).reshape(flat.shape)
    table.wait()

    def source(s, carry):
        spectrum = flat[pl.ds(s, rows, stride=local_src), :].astype(BF16)
        step = tn_dot(jnp.concatenate([spectrum, spectrum], axis=0), synthesis_ref[...])
        done[s] = soft(once_ref[s, pl.ds(start, width), :] + step)
        pltpu.make_async_copy(done.at[s], field_hbm.at[s, pl.ds(start, width), :], done_sem).start()
        return carry

    lax.fori_loop(0, local_src, source, 0, unroll=4)
    pltpu.make_async_copy(done, field_hbm.at[:, pl.ds(start, width), :], done_sem).wait()
    residual.wait()
    if start:
        ready.wait()


def on_device(devices, start_field, recorded, multiples, block_index, radius):
    local_src, receivers, samples = start_field.shape
    local_freq = recorded.shape[0]
    rows = 2 * local_freq * devices
    width = 128
    chunks = receivers // width
    table = dft_table(local_freq * devices, samples)
    analysis = jnp.concatenate(halves(table.T), axis=0)
    high, low = halves(step_size * table.T)
    synthesis = jnp.concatenate([high, low], axis=0)
    side = math.gcd(devices, 8)
    sources = devices * local_src
    vmem = pl.BlockSpec(memory_space=pltpu.VMEM)
    hbm = pl.BlockSpec(memory_space=pltpu.HBM)
    slab = pltpu.VMEM((2 * chunks, devices, local_freq * 2 * local_src, width), BF16)
    flat = pltpu.VMEM((rows * local_src, width), F32)
    field_shape = jax.ShapeDtypeStruct(start_field.shape, F32)
    residual_shape = jax.ShapeDtypeStruct((local_freq, receivers * NB, 2 * BS), F32)
    once, last, residual = pl.pallas_call(
        functools.partial(sweeps_kernel, devices, chunks, width),
        out_shape=(field_shape, jax.ShapeDtypeStruct((devices, local_freq * 2 * local_src, width), BF16), residual_shape),
        in_specs=[hbm] * 7,
        out_specs=(vmem, vmem, vmem),
        scratch_shapes=[
            pltpu.VMEM((chunks, local_src, width, samples), BF16),
            flat,
            flat,
            pltpu.VMEM((2, sources + 2 * PAD, width), F32),
            pltpu.VMEM((chunks, side, devices // side, local_src, width), BF16),
            pltpu.VMEM((sources, receivers), F32),
            pltpu.VMEM((sources, receivers), F32),
            pltpu.VMEM((width * NB, 2 * BS), F32),
            pltpu.VMEM((local_freq, devices * 2 * local_src, NB * 2 * BS), BF16),
            slab,
            slab,
            slab,
            slab,
            pltpu.SMEM(block_index.shape, block_index.dtype),
            pltpu.VMEM((local_freq, receivers * NB, 2 * BS), BF16),
            pltpu.VMEM(multiples.shape, BF16),
            pltpu.VMEM(radius.shape, radius.dtype),
            pltpu.VMEM(analysis.shape, BF16),
            pltpu.VMEM(synthesis.shape, BF16),
            pltpu.SemaphoreType.DMA((chunks,)),
            pltpu.SemaphoreType.DMA((2,)),
            pltpu.SemaphoreType.DMA((4 * chunks,)),
            pltpu.SemaphoreType.DMA((6,)),
            pltpu.SemaphoreType.DMA((3,)),
            pltpu.SemaphoreType.DMA((chunks + 2,)),
        ],
        compiler_params=pltpu.CompilerParams(
            collective_id=0, has_side_effects=True, vmem_limit_bytes=28 << 20
        ),
    )(
        *(
            pltpu.with_memory_space_constraint(value, pltpu.HBM)
            for value in (
                block_index, start_field, recorded.reshape(local_freq, receivers * NB, 2 * BS), multiples, radius,
                analysis, synthesis,
            )
        )
    )
    field, residual = pl.pallas_call(
        finish_kernel,
        out_shape=(field_shape, residual_shape),
        in_specs=[vmem] * 3 + [hbm],
        out_specs=(hbm, hbm),
        scratch_shapes=[
            pltpu.VMEM((local_src, width, samples), F32),
            flat,
            pltpu.VMEM(synthesis.shape, BF16),
            pltpu.SemaphoreType.DMA,
            pltpu.SemaphoreType.DMA,
            pltpu.SemaphoreType.DMA,
            pltpu.SemaphoreType.DMA,
        ],
        compiler_params=pltpu.CompilerParams(vmem_limit_bytes=12 << 20),
    )(once, last, residual, pltpu.with_memory_space_constraint(synthesis, pltpu.HBM))
    return field, residual.reshape(recorded.shape)


def solution(mesh):
    placed = (
        P(("grp", "freq"), None, None),
        P(("grp", "freq"), None, None, None),
        P(("grp", "freq"), None, None, None, None),
        P(),
        P(("grp", "freq"), None),
    )
    return jax.shard_map(
        functools.partial(on_device, mesh.shape["freq"]),
        mesh=mesh,
        in_specs=placed,
        out_specs=(P(("grp", "freq"), None, None), P(("grp", "freq"), None, None, None)),
        check_vma=False,
    )
```
